512 devices in a mesh: dom: 64 (over y, z_hi, x), depth: 8 (over z_lo, core).
Axes of the slice: x: 4, y: 8, z: 8 (z_hi: 2, z_lo: 4; z = z_hi * 4 + z_lo), core: 2. Of those that a mesh axis runs over, the one named last changes fastest.
Arguments:
- ancestors: int32 [64], P('dom'), may hold values from 0 to 63, as said below
- ensemble: float32 [64, 4, 48, 16, 128], P('dom', None, 'depth'), may hold values from -4 to 4
- diffusivity: float32 [48, 16, 128], P('depth'), may hold values from 0.02 to 0.1
- melting_speed: float32 [48, 16, 128], P('depth'), may hold values from 0.05 to 0.3
- permeability: float32 [48, 16, 128], P('depth'), may hold values from 0.5 to 2
Outputs:
- forecast_ensemble: float32 [64, 4, 48, 16, 128], P('dom', None, 'depth')
The draws below stay inside these ranges and needn't reach their ends.
Inputs may be any that keep to these rules, and one draw needn't show every extreme that they name: `ancestors`: each entry names a particle; slots 0 and 2 descend from particle 1, slot 1 from particle 0, slot 3 from particle 64 - 1.
All inputs are finite; a program needn't handle non-finite values.
Results may differ from the reference program's by a relative error of at most 0.00002.
Values sent between devices are 32-bit elements; how exact they have to be, the bound alone decides.
A program may use at most 64 MiB of HBM per device.

```python
import math
import jax
import jax.numpy as jnp
from jax import lax

FIELDS = 4
NX = 16
NY = 128
STEPS = 4
PARTICLES = 64
NZ = 48


def draw_ancestors(key, part):
    key_perm = jax.random.fold_in(key, 11)
    key_first = jax.random.fold_in(key, 12)
    key_second = jax.random.fold_in(key, 13)
    order = jax.random.permutation(key_perm, PARTICLES).astype(jnp.int32)
    first = jax.random.randint(key_first, (PARTICLES,), 0, PARTICLES, dtype=jnp.int32)
    second = jax.random.randint(key_second, (PARTICLES,), 0, PARTICLES, dtype=jnp.int32)
    picked = order[jnp.minimum(first, second)]
    picked = picked.at[0].set(1)
    picked = picked.at[1].set(0)
    picked = picked.at[2].set(1)
    picked = picked.at[3].set(PARTICLES - 1)
    return picked.astype(jnp.int32)


def block_scale(key, shape, shards, smallest, high):
    gain = 1.0
    for axis_at, blocks in shards:
        steps = jax.random.uniform(jax.random.fold_in(jax.random.fold_in(key, 6), axis_at), (blocks,), jnp.float32, smallest / len(shards), high / len(shards))
        gain = gain * jnp.repeat(jnp.exp(steps), shape[axis_at] // blocks).reshape((-1,) + (1,) * (len(shape) - 1 - axis_at))
    return gain


def normal_values(rng, shape, deviation, limit, cuts=(), kind=jnp.bfloat16):
    entries = jax.random.normal(rng, shape, jnp.float32) * deviation
    if len(cuts) > 0:
        entries = block_scale(rng, shape, cuts, -0.22, 0.18) * entries
    return jnp.clip(entries, min=-limit, max=limit).astype(kind)


def setup_inputs(seed: int = 0) -> dict:
    splits = jax.random.split(jax.random.key(seed), 6)
    ancestors = draw_ancestors(jax.random.fold_in(splits[5], 71), 0)
    ensemble = normal_values(splits[1], (PARTICLES, FIELDS, NZ, NX, NY), 1.0, 4.0, ((0, 64), (2, 8)), jnp.float32)
    diffusivity = jnp.clip(jnp.exp(math.log(0.1) - 1.609438 * jax.random.uniform(splits[2], (NZ, NX, NY), jnp.float32) ** block_scale(splits[2], (NZ, NX, NY), ((0, 8),), -0.2, 0.2)), 0.02, 0.1)
    melting_speed = jnp.clip(jnp.exp(math.log(0.3) - 1.7917595 * jax.random.uniform(splits[3], (NZ, NX, NY), jnp.float32) ** block_scale(splits[3], (NZ, NX, NY), ((0, 8),), -0.2, 0.2)), 0.05, 0.3)
    permeability = jnp.clip(jnp.exp(math.log(2.0) - 1.3862944 * jax.random.uniform(splits[4], (NZ, NX, NY), jnp.float32) ** block_scale(splits[4], (NZ, NX, NY), ((0, 8),), -0.2, 0.2)), 0.5, 2.0)
    return dict(ancestors=ancestors, ensemble=ensemble, diffusivity=diffusivity, melting_speed=melting_speed, permeability=permeability)


advect_coef = 0.1


def advance(padded, diffuse, reacts, permeab):
    center = padded[:, :, 1:-1]
    upper_cells = padded[:, :, :-2]
    lower_cells = padded[:, :, 2:]
    flat_pad = jnp.pad(center, ((0, 0), (0, 0), (0, 0), (1, 1), (1, 1)))
    laplacian_operator = upper_cells + lower_cells + flat_pad[:, :, :, 2:, 1:-1] + flat_pad[:, :, :, :-2, 1:-1]
    laplacian_operator = laplacian_operator + flat_pad[:, :, :, 1:-1, 2:] + flat_pad[:, :, :, 1:-1, :-2] - 6.0 * center
    velocity = center[:, 1]
    transport_update = advect_coef * jnp.maximum(velocity, 0.0)[:, None] * (center - upper_cells)
    transport_update = transport_update + advect_coef * jnp.minimum(velocity, 0.0)[:, None] * (lower_cells - center)
    fraction = center[:, 0]
    enthalpy = center[:, 2]
    composition = center[:, 3]
    melting = reacts * (enthalpy - 0.5 * composition)
    new_fraction = fraction - transport_update[:, 0] + melting
    new_velocity = velocity + 0.2 * (permeab * jnp.tanh(fraction) - velocity) + 0.1 * laplacian_operator[:, 1]
    new_enthalpy = enthalpy - transport_update[:, 2] + diffuse * laplacian_operator[:, 2] - 0.5 * melting
    new_composition = composition - transport_update[:, 3] + diffuse * laplacian_operator[:, 3]
    return jnp.stack([new_fraction, new_velocity, new_enthalpy, new_composition], axis=1)


def reference(ancestors, ensemble, diffusivity, melting_speed, permeability):
    present_members = jnp.take(ensemble, ancestors.astype(jnp.int32), axis=0)

    def one_step(step_index, field_stack):
        padded = jnp.pad(field_stack, ((0, 0), (0, 0), (1, 1), (0, 0), (0, 0)))
        return advance(padded, diffusivity, melting_speed, permeability)

    return lax.fori_loop(0, STEPS, one_step, present_members)
```

```python
import functools

import jax
import jax.numpy as jnp
from jax import lax
from jax.experimental import pallas as pl
from jax.experimental.pallas import tpu as pltpu
from jax.sharding import PartitionSpec as P

STEPS = 4
FIELDS = 4
DOM = 64
DEPTH = 8
LAYERS = 6
NX = 16
NY = 128
TILE = 8
TILES = FIELDS * LAYERS * NX // TILE
HALO = STEPS
EXT = LAYERS + 2 * HALO
COEF_HALO = STEPS - 1

advect_coef = 0.1


def remote(src, dst, send_sem, recv_sem, **where):
    return pltpu.make_async_remote_copy(
        src_ref=src,
        dst_ref=dst,
        send_sem=send_sem,
        recv_sem=recv_sem,
        device_id=where,
        device_id_type=pl.DeviceIdType.MESH,
    )


def holder_of(row, i, dp):
    return row * 4 + lax.rem(row + dp + 1 + i, 4)


def resample_kernel(
    anc_ref,
    ens_ref,
    dif_ref,
    spd_ref,
    per_ref,
    state_ref,
    coef_ref,
    held,
    out_tiles,
    anc_send,
    anc_recv,
    anc_row,
    anc_smem,
    anc_sems,
    smem_sem,
    p1_send,
    p1_recv,
    p2_send,
    p2_recv,
    halo_send,
    halo_recv,
    coef_send,
    coef_recv,
):
    me = lax.axis_index("dom")
    dp = lax.axis_index("depth")
    my_row = me // 4
    my_i = lax.rem(lax.rem(me, 4) - my_row - dp - 1 + 64, 4)
    is_holder = my_i != 3
    my_tile = my_row * 3 + my_i
    has_low = dp > 0
    has_high = dp < DEPTH - 1

    barrier = pltpu.get_barrier_semaphore()

    def greet(t, carry):
        pl.semaphore_signal(
            barrier,
            inc=1,
            device_id={"dom": me ^ t},
            device_id_type=pl.DeviceIdType.MESH,
        )
        return carry

    @pl.when(has_low)
    def _():
        pl.semaphore_signal(
            barrier, inc=1, device_id={"depth": dp - 1}, device_id_type=pl.DeviceIdType.MESH
        )

    @pl.when(has_high)
    def _():
        pl.semaphore_signal(
            barrier, inc=1, device_id={"depth": dp + 1}, device_id_type=pl.DeviceIdType.MESH
        )

    lax.fori_loop(1, DOM, greet, 0)
    lane = lax.broadcasted_iota(jnp.int32, (1, 128), 1)
    anc_send[0] = jnp.where(lane == me, anc_ref[0], 0)
    pl.semaphore_wait(
        barrier, DOM - 1 + has_low.astype(jnp.int32) + has_high.astype(jnp.int32)
    )

    def anc_hop(hop, stride):
        def start(t, carry):
            remote(
                anc_send.at[hop],
                anc_recv.at[hop, t],
                anc_sems.at[2 * hop],
                anc_sems.at[2 * hop + 1],
                dom=me ^ (t * stride),
            ).start()
            return carry

        lax.fori_loop(1, 8, start, 0)

    def anc_done(hop):
        view = anc_recv.at[hop, pl.ds(1, 7)]
        pltpu.make_async_copy(view, view, anc_sems.at[2 * hop + 1]).wait()
        total = anc_send[hop]
        for t in range(1, 8):
            total = total + anc_recv[hop, t]
        return total

    anc_hop(0, 8)

    def spread(n, carry):
        row = (n // 3) ^ my_row
        i = lax.rem(n, 3)
        target = holder_of(row, i, dp)
        p = row * 3 + i

        @pl.when(target != me)
        def _():
            remote(ens_ref.at[p], held.at[me], p1_send, p1_recv, dom=target).start()

        @pl.when(target == me)
        def _():
            pltpu.make_async_copy(ens_ref.at[p], held.at[me], p1_send).start()

        return carry

    lax.fori_loop(0, TILES, spread, 0)

    coefs = (dif_ref, spd_ref, per_ref)

    def coef_to_low(c):
        return remote(
            coefs[c].at[pl.ds(0, COEF_HALO)],
            coef_ref.at[1, c],
            coef_send.at[0, c],
            coef_recv.at[1, c],
            depth=dp - 1,
        )

    def coef_to_high(c):
        return remote(
            coefs[c].at[pl.ds(LAYERS - COEF_HALO, COEF_HALO)],
            coef_ref.at[0, c],
            coef_send.at[1, c],
            coef_recv.at[0, c],
            depth=dp + 1,
        )

    anc_send[1] = anc_done(0)
    anc_hop(1, 1)

    @pl.when(has_low)
    def _():
        for c in range(3):
            coef_to_low(c).start()

    @pl.when(has_high)
    def _():
        for c in range(3):
            coef_to_high(c).start()

    anc_row[...] = anc_done(1)
    to_smem = pltpu.make_async_copy(anc_row, anc_smem, smem_sem)
    to_smem.start()
    to_smem.wait()

    state_tiles = state_ref

    f = my_tile // 12
    rest = lax.rem(my_tile, 12)
    layer = rest // 2 + HALO
    half = lax.rem(rest, 2)

    pltpu.make_async_copy(held.at[pl.ds(0, TILES)], held.at[pl.ds(0, TILES)], p1_send).wait()

    @pl.when(is_holder)
    def _():
        pltpu.make_async_copy(
            held.at[pl.ds(0, DOM - 1)], held.at[pl.ds(0, DOM - 1)], p1_recv
        ).wait()
        place = state_tiles.at[f, layer, half]

        def give(t, carry):
            target = me ^ t
            out_tiles[t] = held[anc_smem[0, target]]
            remote(out_tiles.at[t], place, p2_send, p2_recv, dom=target).start()
            return carry

        lax.fori_loop(1, DOM, give, 0)
        out_tiles[0] = held[anc_smem[0, me]]
        pltpu.make_async_copy(out_tiles.at[0], place, p2_recv).start()

    own = held.at[pl.ds(0, TILES)]
    pltpu.make_async_copy(own, own, p2_recv).wait()

    to_low = remote(
        state_ref.at[:, pl.ds(HALO, HALO)],
        state_ref.at[:, pl.ds(HALO + LAYERS, HALO)],
        halo_send.at[0],
        halo_recv.at[1],
        depth=dp - 1,
    )
    to_high = remote(
        state_ref.at[:, pl.ds(LAYERS, HALO)],
        state_ref.at[:, pl.ds(0, HALO)],
        halo_send.at[1],
        halo_recv.at[0],
        depth=dp + 1,
    )

    @pl.when(has_low)
    def _():
        to_low.start()

    @pl.when(has_high)
    def _():
        to_high.start()

    @pl.when(is_holder)
    def _():
        sent = out_tiles.at[pl.ds(1, DOM - 1)]
        pltpu.make_async_copy(sent, sent, p2_send).wait()

    for hop in range(2):
        view = anc_recv.at[hop, pl.ds(1, 7)]
        pltpu.make_async_copy(view, view, anc_sems.at[2 * hop]).wait()

    @pl.when(has_low)
    def _():
        for c in range(3):
            coef_to_low(c).wait_send()
            coef_to_high(c).wait_recv()
        to_low.wait_send()
        to_high.wait_recv()

    @pl.when(has_high)
    def _():
        for c in range(3):
            coef_to_high(c).wait_send()
            coef_to_low(c).wait_recv()
        to_high.wait_send()
        to_low.wait_recv()


def forecast_kernel(state_ref, halo_ref, dif_ref, spd_ref, per_ref, out_ref, a_ref, b_ref):
    dp = lax.axis_index("depth")
    has_low = dp > 0
    has_high = dp < DEPTH - 1
    row = lax.broadcasted_iota(jnp.int32, (NX, NY), 0)
    col = lax.broadcasted_iota(jnp.int32, (NX, NY), 1)
    first_row, last_row = row == 0, row == NX - 1
    first_col, last_col = col == 0, col == NY - 1
    inner = (dif_ref, spd_ref, per_ref)

    def coef(c, e):
        if e < HALO:
            return halo_ref[0, c, e - (HALO - COEF_HALO)]
        if e >= HALO + LAYERS:
            return halo_ref[1, c, e - HALO - LAYERS]
        return inner[c][e - HALO]

    def inside(e, x):
        if e < HALO:
            return jnp.where(has_low, x, 0.0)
        if e >= HALO + LAYERS:
            return jnp.where(has_high, x, 0.0)
        return x

    def flat(x):
        down = jnp.where(first_row, 0.0, pltpu.roll(x, 1, 0))
        up = jnp.where(last_row, 0.0, pltpu.roll(x, NX - 1, 0))
        right = jnp.where(first_col, 0.0, pltpu.roll(x, 1, 1))
        left = jnp.where(last_col, 0.0, pltpu.roll(x, NY - 1, 1))
        return (down + up) + (right + left)

    for step in range(STEPS):
        src = (None, a_ref, b_ref, a_ref)[step]
        dst = (a_ref, b_ref, a_ref, None)[step]

        def load(f, e):
            if src is None:
                return inside(e, state_ref[f, e])
            return src[f, e]

        for e in range(step + 1, EXT - 1 - step):
            m, v, h, c = (load(f, e) for f in range(FIELDS))
            mu, vu, hu, cu = (load(f, e - 1) for f in range(FIELDS))
            ml, vl, hl, cl = (load(f, e + 1) for f in range(FIELDS))
            diffuse, reacts, permeab = coef(0, e), coef(1, e), coef(2, e)
            vp = advect_coef * jnp.maximum(v, 0.0)
            vn = advect_coef * jnp.minimum(v, 0.0)

            def transport(q, qu, ql):
                return vp * (q - qu) + vn * (ql - q)

            def laplace(q, qu, ql):
                return qu + ql + flat(q) - 6.0 * q

            melting = reacts * (h - 0.5 * c)
            new = (
                m - transport(m, mu, ml) + melting,
                v + 0.2 * (permeab * jnp.tanh(m) - v) + 0.1 * laplace(v, vu, vl),
                h - transport(h, hu, hl) + diffuse * laplace(h, hu, hl) - 0.5 * melting,
                c - transport(c, cu, cl) + diffuse * laplace(c, cu, cl),
            )
            for f in range(FIELDS):
                if dst is None:
                    out_ref[f, e - HALO] = new[f]
                else:
                    dst[f, e] = inside(e, new[f])


def local(ancestors, ensemble, diffusivity, melting_speed, permeability):
    any_spec = pl.BlockSpec(memory_space=pl.ANY)
    tiles = ensemble.reshape(TILES, TILE, NY)
    split = (LAYERS, NX // TILE, TILE, NY)
    coefs = [c.reshape(split) for c in (diffusivity, melting_speed, permeability)]
    dma = pltpu.SemaphoreType.DMA
    state, halo = pl.pallas_call(
        resample_kernel,
        out_shape=(
            jax.ShapeDtypeStruct((FIELDS, EXT, NX // TILE, TILE, NY), jnp.float32),
            jax.ShapeDtypeStruct((2, 3, COEF_HALO, NX // TILE, TILE, NY), jnp.float32),
        ),
        in_specs=[pl.BlockSpec(memory_space=pltpu.SMEM)] + [any_spec] * 4,
        out_specs=(any_spec, any_spec),
        scratch_shapes=[
            pltpu.VMEM((DOM, TILE, NY), jnp.float32),
            pltpu.VMEM((DOM, TILE, NY), jnp.float32),
            pltpu.VMEM((2, 1, 128), jnp.int32),
            pltpu.VMEM((2, 8, 1, 128), jnp.int32),
            pltpu.VMEM((1, 128), jnp.int32),
            pltpu.SMEM((1, 128), jnp.int32),
            dma((4,)),
            dma,
            dma,
            dma,
            dma,
            dma,
            dma((2,)),
            dma((2,)),
            dma((2, 3)),
            dma((2, 3)),
        ],
        compiler_params=pltpu.CompilerParams(collective_id=0, has_side_effects=True),
    )(ancestors, tiles, *coefs)
    state = state.reshape(FIELDS, EXT, NX, NY)
    halo = halo.reshape(2, 3, COEF_HALO, NX, NY)
    vmem = pl.BlockSpec(memory_space=pltpu.VMEM)
    out = pl.pallas_call(
        forecast_kernel,
        out_shape=jax.ShapeDtypeStruct((FIELDS, LAYERS, NX, NY), jnp.float32),
        in_specs=[vmem] * 5,
        out_specs=vmem,
        scratch_shapes=[pltpu.VMEM((FIELDS, EXT, NX, NY), jnp.float32)] * 2,
    )(state, halo, diffusivity, melting_speed, permeability)
    return out[None]


def solution(mesh):
    return jax.shard_map(
        local,
        mesh=mesh,
        in_specs=(
            P("dom"),
            P("dom", None, "depth", None, None),
            P("depth", None, None),
            P("depth", None, None),
            P("depth", None, None),
        ),
        out_specs=P("dom", None, "depth", None, None),
        check_vma=False,
    )
```

```python
import jax
import jax.numpy as jnp
from jax import lax
from jax.experimental import pallas as pl
from jax.experimental.pallas import tpu as pltpu
from jax.sharding import PartitionSpec as P

STEPS = 4
FIELDS = 4
DOM = 64
DEPTH = 8
LAYERS = 6
NX = 16
NY = 128
TILE = 8
HOLDERS = FIELDS * LAYERS * NX // TILE
HALO = STEPS
EXT = LAYERS + 2 * HALO
COEF_HALO = STEPS - 1

advect_coef = 0.1


def remote(src, dst, send_sem, recv_sem, **where):
    return pltpu.make_async_remote_copy(
        src_ref=src,
        dst_ref=dst,
        send_sem=send_sem,
        recv_sem=recv_sem,
        device_id=where,
        device_id_type=pl.DeviceIdType.MESH,
    )


def split_dom(index):
    return index // 8, lax.rem(index // 4, 2), lax.rem(index, 4)


def join_dom(y, z_hi, x):
    return y * 8 + z_hi * 4 + x


def resample_kernel(
    anc_ref,
    ens_ref,
    dif_ref,
    spd_ref,
    per_ref,
    state_ref,
    coef_ref,
    held,
    chosen,
    anc_send,
    anc_recv,
    anc_row,
    anc_all,
    anc_sems,
    smem_sem,
    p1_send,
    p1_recv,
    local_sem,
    p2_send,
    p2_recv,
    halo_send,
    halo_recv,
    coef_send,
    coef_recv,
):
    me = lax.axis_index("dom")
    dp = lax.axis_index("depth")
    my_y, my_z, my_x = split_dom(me)
    my_tile = jnp.where(my_z == 0, my_y, DOM // 8 + lax.rem(my_y + 1, 8)) * 4 + my_x
    is_holder = my_tile < HOLDERS
    has_low = dp > 0
    has_high = dp < DEPTH - 1

    barrier = pltpu.get_barrier_semaphore()

    def greet(t, carry):
        pl.semaphore_signal(
            barrier,
            inc=1,
            device_id={"dom": me ^ t},
            device_id_type=pl.DeviceIdType.MESH,
        )
        return carry

    @pl.when(is_holder)
    def _():
        lax.fori_loop(1, DOM, greet, 0)

    @pl.when(jnp.logical_not(is_holder))
    def _():
        for t in range(1, 8):
            greet(t, 0)
            greet(8 * t, 0)

    @pl.when(has_low)
    def _():
        pl.semaphore_signal(
            barrier, inc=1, device_id={"depth": dp - 1}, device_id_type=pl.DeviceIdType.MESH
        )

    @pl.when(has_high)
    def _():
        pl.semaphore_signal(
            barrier, inc=1, device_id={"depth": dp + 1}, device_id_type=pl.DeviceIdType.MESH
        )

    lane = lax.broadcasted_iota(jnp.int32, (1, 128), 1)
    anc_send[0] = jnp.where(lane == me, anc_ref[0], 0)
    other = jnp.where(is_holder, 0, 1)
    far_row = jnp.where((my_y >= 3) & (my_y <= 6), 1, 0)
    pl.semaphore_wait(
        barrier,
        HOLDERS
        - is_holder.astype(jnp.int32)
        + 4 * my_z
        + 4 * far_row
        - 2 * other
        + has_low.astype(jnp.int32)
        + has_high.astype(jnp.int32),
    )

    def anc_hop(hop, stride):
        for t in range(1, 8):
            remote(
                anc_send.at[hop],
                anc_recv.at[hop, t],
                anc_sems.at[2 * hop],
                anc_sems.at[2 * hop + 1],
                dom=me ^ (t * stride),
            ).start()

    def anc_done(hop):
        view = anc_recv.at[hop, pl.ds(1, 7)]
        pltpu.make_async_copy(view, view, anc_sems.at[2 * hop + 1]).wait()
        total = anc_send[hop]
        for t in range(1, 8):
            total = total + anc_recv[hop, t]
        return total

    anc_hop(0, 8)

    turn = 1 - 2 * (dp & 1)

    def spread(z, rows):
        def body(t, carry):
            if z == 0:
                y = (my_y + 8 + t * turn) & 7
                row = y
            else:
                row = 8 + ((my_y + t) & 3)
                y = (row + 7) & 7
            for k in range(4):
                x = my_x ^ k
                p = row * 4 + x
                target = join_dom(y, z, x)

                @pl.when(target != me)
                def _(p=p, target=target):
                    remote(ens_ref.at[p], held.at[me], p1_send, p1_recv, dom=target).start()

            return carry

        lax.fori_loop(0, rows, body, 0)

    @pl.when(my_z == 0)
    def _():
        spread(1, 4)
        spread(0, 8)

    @pl.when(my_z == 1)
    def _():
        spread(0, 8)
        spread(1, 4)

    own_plane = pltpu.make_async_copy(ens_ref.at[my_tile], held.at[me], local_sem.at[0])

    @pl.when(is_holder)
    def _():
        own_plane.start()

    anc_send[1] = anc_done(0)
    anc_hop(1, 1)

    coefs = (dif_ref, spd_ref, per_ref)

    def coef_to_low(c):
        return remote(
            coefs[c].at[pl.ds(0, COEF_HALO)],
            coef_ref.at[1, c],
            coef_send.at[0, c],
            coef_recv.at[1, c],
            depth=dp - 1,
        )

    def coef_to_high(c):
        return remote(
            coefs[c].at[pl.ds(LAYERS - COEF_HALO, COEF_HALO)],
            coef_ref.at[0, c],
            coef_send.at[1, c],
            coef_recv.at[0, c],
            depth=dp + 1,
        )

    @pl.when(has_low)
    def _():
        for c in range(3):
            coef_to_low(c).start()

    @pl.when(has_high)
    def _():
        for c in range(3):
            coef_to_high(c).start()

    anc_row[...] = anc_done(1)
    to_smem = pltpu.make_async_copy(anc_row, anc_all, smem_sem)
    to_smem.start()
    to_smem.wait()

    f = my_tile // (2 * LAYERS)
    layer = HALO + lax.rem(my_tile, 2 * LAYERS) // 2
    half = lax.rem(my_tile, 2)

    @pl.when(is_holder)
    def _():
        others = held.at[pl.ds(0, DOM - 1)]
        pltpu.make_async_copy(others, others, p1_recv).wait()
        own_plane.wait()
        place = state_ref.at[f, layer, half]

        def give(z):
            def body(t, carry):
                y = (my_y + 8 + t * turn) & 7
                for k in range(4):
                    n = z * 32 + t * 4 + k
                    target = join_dom(y, z, my_x ^ k)
                    chosen[n] = held[anc_all[0, target]]

                    @pl.when(target != me)
                    def _(n=n, target=target):
                        remote(chosen.at[n], place, p2_send, p2_recv, dom=target).start()

                    @pl.when(target == me)
                    def _(n=n):
                        pltpu.make_async_copy(chosen.at[n], place, p2_recv).start()

                return carry

            lax.fori_loop(0, 8, body, 0)

        give(0)
        give(1)

    own = held.at[pl.ds(0, HOLDERS)]
    pltpu.make_async_copy(own, own, p2_recv).wait()

    to_low = remote(
        state_ref.at[:, pl.ds(HALO, HALO)],
        state_ref.at[:, pl.ds(HALO + LAYERS, HALO)],
        halo_send.at[0],
        halo_recv.at[1],
        depth=dp - 1,
    )
    to_high = remote(
        state_ref.at[:, pl.ds(LAYERS, HALO)],
        state_ref.at[:, pl.ds(0, HALO)],
        halo_send.at[1],
        halo_recv.at[0],
        depth=dp + 1,
    )

    @pl.when(has_low)
    def _():
        to_low.start()

    @pl.when(has_high)
    def _():
        to_high.start()

    @pl.when(is_holder)
    def _():
        sent = held.at[pl.ds(0, HOLDERS - 1)]
        pltpu.make_async_copy(sent, sent, p1_send).wait()
        sent = chosen.at[pl.ds(0, DOM - 1)]
        pltpu.make_async_copy(sent, sent, p2_send).wait()

    @pl.when(jnp.logical_not(is_holder))
    def _():
        sent = held.at[pl.ds(0, HOLDERS)]
        pltpu.make_async_copy(sent, sent, p1_send).wait()

    for hop in range(2):
        view = anc_recv.at[hop, pl.ds(1, 7)]
        pltpu.make_async_copy(view, view, anc_sems.at[2 * hop]).wait()

    @pl.when(has_low)
    def _():
        for c in range(3):
            coef_to_low(c).wait_send()
            coef_to_high(c).wait_recv()
        to_low.wait_send()
        to_high.wait_recv()

    @pl.when(has_high)
    def _():
        for c in range(3):
            coef_to_high(c).wait_send()
            coef_to_low(c).wait_recv()
        to_high.wait_send()
        to_low.wait_recv()


def forecast_kernel(state_ref, halo_ref, dif_ref, spd_ref, per_ref, out_ref, a_ref, b_ref):
    dp = lax.axis_index("depth")
    has_low = dp > 0
    has_high = dp < DEPTH - 1
    row = lax.broadcasted_iota(jnp.int32, (NX, NY), 0)
    col = lax.broadcasted_iota(jnp.int32, (NX, NY), 1)
    first_row, last_row = row == 0, row == NX - 1
    first_col, last_col = col == 0, col == NY - 1
    inner = (dif_ref, spd_ref, per_ref)

    def coef(c, e):
        if e < HALO:
            return halo_ref[0, c, e - (HALO - COEF_HALO)]
        if e >= HALO + LAYERS:
            return halo_ref[1, c, e - HALO - LAYERS]
        return inner[c][e - HALO]

    def inside(e, x):
        if e < HALO:
            return jnp.where(has_low, x, 0.0)
        if e >= HALO + LAYERS:
            return jnp.where(has_high, x, 0.0)
        return x

    def flat(x):
        down = jnp.where(first_row, 0.0, pltpu.roll(x, 1, 0))
        up = jnp.where(last_row, 0.0, pltpu.roll(x, NX - 1, 0))
        right = jnp.where(first_col, 0.0, pltpu.roll(x, 1, 1))
        left = jnp.where(last_col, 0.0, pltpu.roll(x, NY - 1, 1))
        return (down + up) + (right + left)

    for step in range(STEPS):
        src = (None, a_ref, b_ref, a_ref)[step]
        dst = (a_ref, b_ref, a_ref, None)[step]

        def load(f, e):
            if src is None:
                return inside(e, state_ref[f, e])
            return src[f, e]

        for e in range(step + 1, EXT - 1 - step):
            m, v, h, c = (load(f, e) for f in range(FIELDS))
            mu, vu, hu, cu = (load(f, e - 1) for f in range(FIELDS))
            ml, vl, hl, cl = (load(f, e + 1) for f in range(FIELDS))
            diffuse, reacts, permeab = coef(0, e), coef(1, e), coef(2, e)
            vp = advect_coef * jnp.maximum(v, 0.0)
            vn = advect_coef * jnp.minimum(v, 0.0)

            def transport(q, qu, ql):
                return vp * (q - qu) + vn * (ql - q)

            def laplace(q, qu, ql):
                return qu + ql + flat(q) - 6.0 * q

            melting = reacts * (h - 0.5 * c)
            new = (
                m - transport(m, mu, ml) + melting,
                v + 0.2 * (permeab * jnp.tanh(m) - v) + 0.1 * laplace(v, vu, vl),
                h - transport(h, hu, hl) + diffuse * laplace(h, hu, hl) - 0.5 * melting,
                c - transport(c, cu, cl) + diffuse * laplace(c, cu, cl),
            )
            for f in range(FIELDS):
                if dst is None:
                    out_ref[f, e - HALO] = new[f]
                else:
                    dst[f, e] = inside(e, new[f])


def local(ancestors, ensemble, diffusivity, melting_speed, permeability):
    any_spec = pl.BlockSpec(memory_space=pl.ANY)
    tiles = ensemble.reshape(HOLDERS, TILE, NY)
    split = (LAYERS, NX // TILE, TILE, NY)
    coefs = [c.reshape(split) for c in (diffusivity, melting_speed, permeability)]
    dma = pltpu.SemaphoreType.DMA
    state, halo = pl.pallas_call(
        resample_kernel,
        out_shape=(
            jax.ShapeDtypeStruct((FIELDS, EXT, NX // TILE, TILE, NY), jnp.float32),
            jax.ShapeDtypeStruct((2, 3, COEF_HALO, NX // TILE, TILE, NY), jnp.float32),
        ),
        in_specs=[pl.BlockSpec(memory_space=pltpu.SMEM)] + [any_spec] * 4,
        out_specs=(any_spec, any_spec),
        scratch_shapes=[
            pltpu.VMEM((DOM, TILE, NY), jnp.float32),
            pltpu.VMEM((DOM, TILE, NY), jnp.float32),
            pltpu.VMEM((2, 1, 128), jnp.int32),
            pltpu.VMEM((2, 8, 1, 128), jnp.int32),
            pltpu.VMEM((1, 128), jnp.int32),
            pltpu.SMEM((1, 128), jnp.int32),
            dma((4,)),
            dma,
            dma,
            dma,
            dma((1,)),
            dma,
            dma,
            dma((2,)),
            dma((2,)),
            dma((2, 3)),
            dma((2, 3)),
        ],
        compiler_params=pltpu.CompilerParams(collective_id=0, has_side_effects=True),
    )(ancestors, tiles, *coefs)
    state = state.reshape(FIELDS, EXT, NX, NY)
    halo = halo.reshape(2, 3, COEF_HALO, NX, NY)
    vmem = pl.BlockSpec(memory_space=pltpu.VMEM)
    out = pl.pallas_call(
        forecast_kernel,
        out_shape=jax.ShapeDtypeStruct((FIELDS, LAYERS, NX, NY), jnp.float32),
        in_specs=[vmem] * 5,
        out_specs=vmem,
        scratch_shapes=[pltpu.VMEM((FIELDS, EXT, NX, NY), jnp.float32)] * 2,
    )(state, halo, diffusivity, melting_speed, permeability)
    return out[None]


def solution(mesh):
    return jax.shard_map(
        local,
        mesh=mesh,
        in_specs=(
            P("dom"),
            P("dom", None, "depth", None, None),
            P("depth", None, None),
            P("depth", None, None),
            P("depth", None, None),
        ),
        out_specs=P("dom", None, "depth", None, None),
        check_vma=False,
    )
```

```python
import jax
import jax.numpy as jnp
from jax import lax
from jax.experimental import pallas as pl
from jax.experimental.pallas import tpu as pltpu
from jax.sharding import PartitionSpec as P

STEPS = 4
FIELDS = 4
DOM = 64
DEPTH = 8
LAYERS = 6
NX = 16
NY = 128
TILE = 8
HOLDERS = FIELDS * LAYERS * NX // TILE
HALO = STEPS
EXT = LAYERS + 2 * HALO
COEF_HALO = STEPS - 1

advect_coef = 0.1


def remote(src, dst, send_sem, recv_sem, **where):
    return pltpu.make_async_remote_copy(
        src_ref=src,
        dst_ref=dst,
        send_sem=send_sem,
        recv_sem=recv_sem,
        device_id=where,
        device_id_type=pl.DeviceIdType.MESH,
    )


def split_dom(index):
    return index // 8, lax.rem(index // 4, 2), lax.rem(index, 4)


def join_dom(y, z_hi, x):
    return y * 8 + z_hi * 4 + x


def resample_kernel(
    anc_ref,
    ens_ref,
    dif_ref,
    spd_ref,
    per_ref,
    state_ref,
    coef_ref,
    held,
    chosen,
    mine,
    mine_sem,
    anc_send,
    anc_recv,
    anc_row,
    anc_all,
    anc_sems,
    smem_sem,
    p1_send,
    p1_recv,
    local_sem,
    p2_send,
    p2_recv,
    halo_send,
    halo_recv,
    coef_send,
    coef_recv,
    own_coef_sem,
):
    me = lax.axis_index("dom")
    dp = lax.axis_index("depth")
    my_y, my_z, my_x = split_dom(me)
    near = (my_y + 2) & 7
    late_holder = ((my_x != 2) & (near < 5)) | ((my_x == 2) & (my_y == 0))
    late_tile = jnp.where(my_x == 2, HOLDERS - 1, DOM // 2 + near * 3 + my_x - my_x // 3)
    my_tile = jnp.where(my_z == 0, my_y * 4 + my_x, late_tile)
    is_holder = (my_z == 0) | late_holder
    has_low = dp > 0
    has_high = dp < DEPTH - 1

    fetch = pltpu.make_async_copy(ens_ref, mine, mine_sem)
    fetch.start()
    coefs = (dif_ref, spd_ref, per_ref)
    own_coefs = [
        pltpu.make_async_copy(
            coefs[c], coef_ref.at[c, pl.ds(COEF_HALO, LAYERS)], own_coef_sem.at[c]
        )
        for c in range(3)
    ]
    barrier = pltpu.get_barrier_semaphore()

    def greet(t, carry):
        pl.semaphore_signal(
            barrier,
            inc=1,
            device_id={"dom": me ^ t},
            device_id_type=pl.DeviceIdType.MESH,
        )
        return carry

    @pl.when(is_holder)
    def _():
        def greet_row(t, carry):
            for z in (1, 0):
                for k in range(4):
                    greet(t * 8 + z * 4 + k, 0)
            return carry

        for t in (4, 5, 3, 6, 2, 7, 1):
            greet_row(t, 0)
        for k in range(4):
            greet(4 + k, 0)
        for k in range(1, 4):
            greet(k, 0)

    @pl.when(jnp.logical_not(is_holder))
    def _():
        for t in range(1, 8):
            greet(t, 0)
            greet(8 * t, 0)

    @pl.when(has_low)
    def _():
        pl.semaphore_signal(
            barrier, inc=1, device_id={"depth": dp - 1}, device_id_type=pl.DeviceIdType.MESH
        )

    @pl.when(has_high)
    def _():
        pl.semaphore_signal(
            barrier, inc=1, device_id={"depth": dp + 1}, device_id_type=pl.DeviceIdType.MESH
        )

    lane = lax.broadcasted_iota(jnp.int32, (1, 128), 1)
    anc_send[0] = jnp.where(lane == me, anc_ref[0], 0)
    other = jnp.where(is_holder, 0, 1)
    column = my_z * jnp.where(my_x == 2, 7, 3)
    row = jnp.where(my_y == 0, 0, jnp.where(near < 5, 1, 4))
    pl.semaphore_wait(
        barrier,
        HOLDERS
        - is_holder.astype(jnp.int32)
        + column
        + row
        - 2 * other
        + has_low.astype(jnp.int32)
        + has_high.astype(jnp.int32),
    )

    def anc_hop(hop, stride):
        for t in range(1, 8):
            remote(
                anc_send.at[hop],
                anc_recv.at[hop, t],
                anc_sems.at[2 * hop],
                anc_sems.at[2 * hop + 1],
                dom=me ^ (t * stride),
            ).start()

    def anc_done(hop):
        view = anc_recv.at[hop, pl.ds(1, 7)]
        pltpu.make_async_copy(view, view, anc_sems.at[2 * hop + 1]).wait()
        total = anc_send[hop]
        for t in range(1, 8):
            total = total + anc_recv[hop, t]
        return total

    anc_hop(0, 8)
    fetch.wait()

    turn = 1 - 2 * (dp & 1)

    def send_tile(p, target):
        @pl.when(target != me)
        def _():
            remote(mine.at[p], held.at[me], p1_send, p1_recv, dom=target).start()

    def spread_early():
        def body(t, carry):
            y = (my_y + 12 + t * turn) & 7
            for k in range(4):
                x = my_x ^ k
                send_tile(y * 4 + x, join_dom(y, 0, x))
            return carry

        lax.fori_loop(0, 8, body, 0)

    def spread_late():
        def body(t, carry):
            for i in range(3):
                send_tile(DOM // 2 + t * 3 + i, join_dom((t + 6) & 7, 1, i + i // 2))
            return carry

        lax.fori_loop(0, 5, body, 0)
        send_tile(HOLDERS - 1, join_dom(0, 1, 2))

    @pl.when(my_z == 0)
    def _():
        spread_late()
        spread_early()

    @pl.when(my_z == 1)
    def _():
        spread_early()
        spread_late()

    own_plane = pltpu.make_async_copy(mine.at[my_tile], held.at[me], local_sem.at[0])

    @pl.when(is_holder)
    def _():
        own_plane.start()

    anc_send[1] = anc_done(0)
    anc_hop(1, 1)
    for copy in own_coefs:
        copy.start()


    def coef_to_low(c):
        return remote(
            coefs[c].at[pl.ds(0, COEF_HALO)],
            coef_ref.at[c, pl.ds(COEF_HALO + LAYERS, COEF_HALO)],
            coef_send.at[0, c],
            coef_recv.at[1, c],
            depth=dp - 1,
        )

    def coef_to_high(c):
        return remote(
            coefs[c].at[pl.ds(LAYERS - COEF_HALO, COEF_HALO)],
            coef_ref.at[c, pl.ds(0, COEF_HALO)],
            coef_send.at[1, c],
            coef_recv.at[0, c],
            depth=dp + 1,
        )

    @pl.when(has_low)
    def _():
        for c in range(3):
            coef_to_low(c).start()

    @pl.when(has_high)
    def _():
        for c in range(3):
            coef_to_high(c).start()

    anc_row[...] = anc_done(1)
    to_smem = pltpu.make_async_copy(anc_row, anc_all, smem_sem)
    to_smem.start()
    to_smem.wait()

    f = my_tile // (2 * LAYERS)
    layer = HALO + lax.rem(my_tile, 2 * LAYERS) // 2
    half = lax.rem(my_tile, 2)

    @pl.when(is_holder)
    def _():
        others = held.at[pl.ds(0, DOM - 1)]
        pltpu.make_async_copy(others, others, p1_recv).wait()
        own_plane.wait()
        place = state_ref.at[f, layer, half]

        def give(z):
            def body(t, carry):
                y = (my_y + 8 + t * turn) & 7
                for k in range(4):
                    n = z * 32 + t * 4 + k
                    target = join_dom(y, z, my_x ^ k)
                    chosen[n] = held[anc_all[0, target]]

                    @pl.when(target != me)
                    def _(n=n, target=target):
                        remote(chosen.at[n], place, p2_send, p2_recv.at[f], dom=target).start()

                    @pl.when(target == me)
                    def _(n=n):
                        pltpu.make_async_copy(chosen.at[n], place, p2_recv.at[f]).start()

                return carry

            lax.fori_loop(0, 8, body, 0)

        give(0)
        give(1)

    def to_low(field):
        return remote(
            state_ref.at[field, pl.ds(HALO, HALO)],
            state_ref.at[field, pl.ds(HALO + LAYERS, HALO)],
            halo_send.at[0, field],
            halo_recv.at[1, field],
            depth=dp - 1,
        )

    def to_high(field):
        return remote(
            state_ref.at[field, pl.ds(LAYERS, HALO)],
            state_ref.at[field, pl.ds(0, HALO)],
            halo_send.at[1, field],
            halo_recv.at[0, field],
            depth=dp + 1,
        )

    for field in range(FIELDS):
        own = held.at[pl.ds(0, HOLDERS // FIELDS)]
        pltpu.make_async_copy(own, own, p2_recv.at[field]).wait()

        @pl.when(has_low)
        def _(field=field):
            to_low(field).start()

        @pl.when(has_high)
        def _(field=field):
            to_high(field).start()

    @pl.when(is_holder)
    def _():
        sent = held.at[pl.ds(0, HOLDERS - 1)]
        pltpu.make_async_copy(sent, sent, p1_send).wait()
        sent = chosen.at[pl.ds(0, DOM - 1)]
        pltpu.make_async_copy(sent, sent, p2_send).wait()

    @pl.when(jnp.logical_not(is_holder))
    def _():
        sent = held.at[pl.ds(0, HOLDERS)]
        pltpu.make_async_copy(sent, sent, p1_send).wait()

    for copy in own_coefs:
        copy.wait()

    for hop in range(2):
        view = anc_recv.at[hop, pl.ds(1, 7)]
        pltpu.make_async_copy(view, view, anc_sems.at[2 * hop]).wait()

    @pl.when(has_low)
    def _():
        for c in range(3):
            coef_to_low(c).wait_send()
            coef_to_high(c).wait_recv()
        for field in range(FIELDS):
            to_low(field).wait_send()
            to_high(field).wait_recv()

    @pl.when(has_high)
    def _():
        for c in range(3):
            coef_to_high(c).wait_send()
            coef_to_low(c).wait_recv()
        for field in range(FIELDS):
            to_high(field).wait_send()
            to_low(field).wait_recv()


def forecast_kernel(state_ref, coef_ref, out_ref, a_ref, b_ref):
    dp = lax.axis_index("depth")
    has_low = dp > 0
    has_high = dp < DEPTH - 1
    row = lax.broadcasted_iota(jnp.int32, (NX, NY), 0)
    col = lax.broadcasted_iota(jnp.int32, (NX, NY), 1)
    first_row, last_row = row == 0, row == NX - 1
    first_col, last_col = col == 0, col == NY - 1

    def coef(c, e):
        return coef_ref[c, e - (HALO - COEF_HALO)]

    def inside(e, x):
        if e < HALO:
            return jnp.where(has_low, x, 0.0)
        if e >= HALO + LAYERS:
            return jnp.where(has_high, x, 0.0)
        return x

    def flat(x):
        down = jnp.where(first_row, 0.0, pltpu.roll(x, 1, 0))
        up = jnp.where(last_row, 0.0, pltpu.roll(x, NX - 1, 0))
        right = jnp.where(first_col, 0.0, pltpu.roll(x, 1, 1))
        left = jnp.where(last_col, 0.0, pltpu.roll(x, NY - 1, 1))
        return (down + up) + (right + left)

    for step in range(STEPS):
        src = (None, a_ref, b_ref, a_ref)[step]
        dst = (a_ref, b_ref, a_ref, None)[step]

        def load(f, e):
            if src is None:
                return inside(e, state_ref[f, e])
            return src[f, e]

        for e in range(step + 1, EXT - 1 - step):
            m, v, h, c = (load(f, e) for f in range(FIELDS))
            mu, vu, hu, cu = (load(f, e - 1) for f in range(FIELDS))
            ml, vl, hl, cl = (load(f, e + 1) for f in range(FIELDS))
            diffuse, reacts, permeab = coef(0, e), coef(1, e), coef(2, e)
            vp = advect_coef * jnp.maximum(v, 0.0)
            vn = advect_coef * jnp.minimum(v, 0.0)

            def transport(q, qu, ql):
                return vp * (q - qu) + vn * (ql - q)

            def laplace(q, qu, ql):
                return qu + ql + flat(q) - 6.0 * q

            melting = reacts * (h - 0.5 * c)
            new = (
                m - transport(m, mu, ml) + melting,
                v + 0.2 * (permeab * jnp.tanh(m) - v) + 0.1 * laplace(v, vu, vl),
                h - transport(h, hu, hl) + diffuse * laplace(h, hu, hl) - 0.5 * melting,
                c - transport(c, cu, cl) + diffuse * laplace(c, cu, cl),
            )
            for f in range(FIELDS):
                if dst is None:
                    out_ref[f, e - HALO] = new[f]
                else:
                    dst[f, e] = inside(e, new[f])


def local(ancestors, ensemble, diffusivity, melting_speed, permeability):
    any_spec = pl.BlockSpec(memory_space=pl.ANY)
    tiles = ensemble.reshape(HOLDERS, TILE, NY)
    split = (LAYERS, NX // TILE, TILE, NY)
    coefs = [c.reshape(split) for c in (diffusivity, melting_speed, permeability)]
    dma = pltpu.SemaphoreType.DMA
    state, coefs = pl.pallas_call(
        resample_kernel,
        out_shape=(
            pltpu.VMEM((FIELDS, EXT, NX // TILE, TILE, NY), jnp.float32),
            pltpu.VMEM((3, LAYERS + 2 * COEF_HALO, NX // TILE, TILE, NY), jnp.float32),
        ),
        in_specs=[pl.BlockSpec(memory_space=pltpu.SMEM)] + [any_spec] * 4,
        out_specs=(pl.BlockSpec(memory_space=pltpu.VMEM),) * 2,
        scratch_shapes=[
            pltpu.VMEM((DOM, TILE, NY), jnp.float32),
            pltpu.VMEM((DOM, TILE, NY), jnp.float32),
            pltpu.VMEM((HOLDERS, TILE, NY), jnp.float32),
            dma,
            pltpu.VMEM((2, 1, 128), jnp.int32),
            pltpu.VMEM((2, 8, 1, 128), jnp.int32),
            pltpu.VMEM((1, 128), jnp.int32),
            pltpu.SMEM((1, 128), jnp.int32),
            dma((4,)),
            dma,
            dma,
            dma,
            dma((1,)),
            dma,
            dma((FIELDS,)),
            dma((2, FIELDS)),
            dma((2, FIELDS)),
            dma((2, 3)),
            dma((2, 3)),
            dma((3,)),
        ],
        compiler_params=pltpu.CompilerParams(collective_id=0, has_side_effects=True),
    )(ancestors, tiles, *coefs)
    state = state.reshape(FIELDS, EXT, NX, NY)
    coefs = coefs.reshape(3, LAYERS + 2 * COEF_HALO, NX, NY)
    vmem = pl.BlockSpec(memory_space=pltpu.VMEM)
    pin, space = pltpu.with_memory_space_constraint, pltpu.VMEM
    out = pl.pallas_call(
        forecast_kernel,
        out_shape=jax.ShapeDtypeStruct((FIELDS, LAYERS, NX, NY), jnp.float32),
        in_specs=[vmem] * 2,
        out_specs=vmem,
        scratch_shapes=[pltpu.VMEM((FIELDS, EXT, NX, NY), jnp.float32)] * 2,
    )(pin(state, space), pin(coefs, space))
    return out[None]


def solution(mesh):
    return jax.shard_map(
        local,
        mesh=mesh,
        in_specs=(
            P("dom"),
            P("dom", None, "depth", None, None),
            P("depth", None, None),
            P("depth", None, None),
            P("depth", None, None),
        ),
        out_specs=P("dom", None, "depth", None, None),
        check_vma=False,
    )
```

```python
import jax
import jax.numpy as jnp
from jax import lax
from jax.experimental import pallas as pl
from jax.experimental.pallas import tpu as pltpu
from jax.sharding import PartitionSpec as P

STEPS = 4
FIELDS = 4
DOM = 64
DEPTH = 8
LAYERS = 6
NX = 16
NY = 128
TILE = 8
HOLDERS = FIELDS * LAYERS * NX // TILE
HALO = STEPS
EXT = LAYERS + 2 * HALO
COEF_HALO = STEPS - 1

advect_coef = 0.1


def remote(src, dst, send_sem, recv_sem, **where):
    return pltpu.make_async_remote_copy(
        src_ref=src,
        dst_ref=dst,
        send_sem=send_sem,
        recv_sem=recv_sem,
        device_id=where,
        device_id_type=pl.DeviceIdType.MESH,
    )


def split_dom(index):
    return index // 8, lax.rem(index // 4, 2), lax.rem(index, 4)


def join_dom(y, z_hi, x):
    return y * 8 + z_hi * 4 + x


def resample_kernel(
    anc_ref,
    ens_ref,
    dif_ref,
    spd_ref,
    per_ref,
    state_ref,
    coef_ref,
    held,
    chosen,
    mine,
    mine_sem,
    anc_send,
    anc_recv,
    anc_row,
    anc_all,
    anc_sems,
    smem_sem,
    p1_send,
    p1_recv,
    local_sem,
    p2_send,
    p2_recv,
    halo_send,
    halo_recv,
    coef_send,
    coef_recv,
    own_coef_sem,
    cross,
):
    me = lax.axis_index("dom")
    dp = lax.axis_index("depth")
    my_y, my_z, my_x = split_dom(me)
    near = (my_y + 2) & 7
    late_holder = ((my_x != 2) & (near < 5)) | ((my_x == 2) & (my_y == 0))
    late_tile = jnp.where(my_x == 2, HOLDERS - 1, DOM // 2 + near * 3 + my_x - my_x // 3)
    my_tile = jnp.where(my_z == 0, my_y * 4 + my_x, late_tile)
    is_holder = (my_z == 0) | late_holder
    has_low = dp > 0
    has_high = dp < DEPTH - 1

    fetch = pltpu.make_async_copy(ens_ref, mine, mine_sem)
    fetch.start()
    coefs = (dif_ref, spd_ref, per_ref)
    own_coefs = [
        pltpu.make_async_copy(
            coefs[c], coef_ref.at[c, pl.ds(COEF_HALO, LAYERS)], own_coef_sem.at[c]
        )
        for c in range(3)
    ]
    barrier = pltpu.get_barrier_semaphore()

    def greet(t, carry):
        pl.semaphore_signal(
            barrier,
            inc=1,
            device_id={"dom": me ^ t},
            device_id_type=pl.DeviceIdType.MESH,
        )
        return carry

    for t in (4, 5, 3, 6, 2, 7, 1):
        greet(8 * t, 0)
    for t in (2, 3, 1):
        greet(t, 0)

    @pl.when(my_z == 0)
    def _():
        def greet_late(t, carry):
            for k in range(4):
                greet(t * 8 + 4 + k, 0)
            return carry

        lax.fori_loop(0, 8, greet_late, 0)

    @pl.when(has_low)
    def _():
        pl.semaphore_signal(
            barrier, inc=1, device_id={"depth": dp - 1}, device_id_type=pl.DeviceIdType.MESH
        )

    @pl.when(has_high)
    def _():
        pl.semaphore_signal(
            barrier, inc=1, device_id={"depth": dp + 1}, device_id_type=pl.DeviceIdType.MESH
        )

    lane = lax.broadcasted_iota(jnp.int32, (1, 128), 1)
    anc_send[0] = jnp.where(lane == me, anc_ref[0], 0)
    pl.semaphore_wait(
        barrier,
        10
        + DOM // 2 * my_z
        + has_low.astype(jnp.int32)
        + has_high.astype(jnp.int32),
    )

    def anc_hop(hop, stride):
        for t in range(1, 8):
            remote(
                anc_send.at[hop],
                anc_recv.at[hop, t],
                anc_sems.at[2 * hop],
                anc_sems.at[2 * hop + 1],
                dom=me ^ (t * stride),
            ).start()

    def anc_done(hop):
        view = anc_recv.at[hop, pl.ds(1, 7)]
        pltpu.make_async_copy(view, view, anc_sems.at[2 * hop + 1]).wait()
        total = anc_send[hop]
        for t in range(1, 8):
            total = total + anc_recv[hop, t]
        return total

    anc_hop(0, 8)

    turn = 1 - 2 * (dp & 1)

    def send_tile(p, target):
        @pl.when(target != me)
        def _():
            remote(mine.at[p], held.at[me], p1_send, p1_recv, dom=target).start()

    def spread_early():
        def body(t, carry):
            y = (my_y + 12 + t * turn) & 7
            for k in range(4):
                x = my_x ^ k
                send_tile(y * 4 + x, join_dom(y, 0, x))
            return carry

        lax.fori_loop(0, 8, body, 0)

    def spread_late():
        def body(t, carry):
            for i in range(3):
                send_tile(DOM // 2 + t * 3 + i, join_dom((t + 6) & 7, 1, i + i // 2))
            return carry

        lax.fori_loop(0, 5, body, 0)
        send_tile(HOLDERS - 1, join_dom(0, 1, 2))

    fetch.wait()

    @pl.when(my_z == 1)
    def _():
        for k in range(4):
            pl.semaphore_signal(
                cross,
                inc=1,
                device_id={"dom": me ^ (4 + k)},
                device_id_type=pl.DeviceIdType.MESH,
            )
        spread_early()

    anc_send[1] = anc_done(0)

    @pl.when(my_z == 0)
    def _():
        spread_early()
        pl.semaphore_wait(cross, 4)

    anc_hop(1, 1)
    spread_late()

    own_plane = pltpu.make_async_copy(mine.at[my_tile], held.at[me], local_sem.at[0])

    @pl.when(is_holder)
    def _():
        own_plane.start()

    for copy in own_coefs:
        copy.start()


    def coef_to_low(c):
        return remote(
            coefs[c].at[pl.ds(0, COEF_HALO)],
            coef_ref.at[c, pl.ds(COEF_HALO + LAYERS, COEF_HALO)],
            coef_send.at[0, c],
            coef_recv.at[1, c],
            depth=dp - 1,
        )

    def coef_to_high(c):
        return remote(
            coefs[c].at[pl.ds(LAYERS - COEF_HALO, COEF_HALO)],
            coef_ref.at[c, pl.ds(0, COEF_HALO)],
            coef_send.at[1, c],
            coef_recv.at[0, c],
            depth=dp + 1,
        )

    @pl.when(has_low)
    def _():
        for c in range(3):
            coef_to_low(c).start()

    @pl.when(has_high)
    def _():
        for c in range(3):
            coef_to_high(c).start()

    anc_row[...] = anc_done(1)
    to_smem = pltpu.make_async_copy(anc_row, anc_all, smem_sem)
    to_smem.start()
    to_smem.wait()

    f = my_tile // (2 * LAYERS)
    layer = HALO + lax.rem(my_tile, 2 * LAYERS) // 2
    half = lax.rem(my_tile, 2)

    @pl.when(is_holder)
    def _():
        others = held.at[pl.ds(0, DOM - 1)]
        pltpu.make_async_copy(others, others, p1_recv).wait()
        own_plane.wait()
        place = state_ref.at[f, layer, half]

        def give(z):
            def body(t, carry):
                y = (my_y + 8 + t * turn) & 7
                for k in range(4):
                    n = z * 32 + t * 4 + k
                    target = join_dom(y, z, my_x ^ k)
                    chosen[n] = held[anc_all[0, target]]

                    @pl.when(target != me)
                    def _(n=n, target=target):
                        remote(chosen.at[n], place, p2_send, p2_recv.at[f], dom=target).start()

                    @pl.when(target == me)
                    def _(n=n):
                        pltpu.make_async_copy(chosen.at[n], place, p2_recv.at[f]).start()

                return carry

            lax.fori_loop(0, 8, body, 0)

        give(0)
        give(1)

    def to_low(field):
        return remote(
            state_ref.at[field, pl.ds(HALO, HALO)],
            state_ref.at[field, pl.ds(HALO + LAYERS, HALO)],
            halo_send.at[0, field],
            halo_recv.at[1, field],
            depth=dp - 1,
        )

    def to_high(field):
        return remote(
            state_ref.at[field, pl.ds(LAYERS, HALO)],
            state_ref.at[field, pl.ds(0, HALO)],
            halo_send.at[1, field],
            halo_recv.at[0, field],
            depth=dp + 1,
        )

    for field in range(FIELDS):
        own = held.at[pl.ds(0, HOLDERS // FIELDS)]
        pltpu.make_async_copy(own, own, p2_recv.at[field]).wait()

        @pl.when(has_low)
        def _(field=field):
            to_low(field).start()

        @pl.when(has_high)
        def _(field=field):
            to_high(field).start()

    @pl.when(is_holder)
    def _():
        sent = held.at[pl.ds(0, HOLDERS - 1)]
        pltpu.make_async_copy(sent, sent, p1_send).wait()
        sent = chosen.at[pl.ds(0, DOM - 1)]
        pltpu.make_async_copy(sent, sent, p2_send).wait()

    @pl.when(jnp.logical_not(is_holder))
    def _():
        sent = held.at[pl.ds(0, HOLDERS)]
        pltpu.make_async_copy(sent, sent, p1_send).wait()

    for copy in own_coefs:
        copy.wait()

    for hop in range(2):
        view = anc_recv.at[hop, pl.ds(1, 7)]
        pltpu.make_async_copy(view, view, anc_sems.at[2 * hop]).wait()

    @pl.when(has_low)
    def _():
        for c in range(3):
            coef_to_low(c).wait_send()
            coef_to_high(c).wait_recv()
        for field in range(FIELDS):
            to_low(field).wait_send()
            to_high(field).wait_recv()

    @pl.when(has_high)
    def _():
        for c in range(3):
            coef_to_high(c).wait_send()
            coef_to_low(c).wait_recv()
        for field in range(FIELDS):
            to_high(field).wait_send()
            to_low(field).wait_recv()


def forecast_kernel(state_ref, coef_ref, out_ref, a_ref, b_ref):
    dp = lax.axis_index("depth")
    has_low = dp > 0
    has_high = dp < DEPTH - 1
    row = lax.broadcasted_iota(jnp.int32, (NX, NY), 0)
    col = lax.broadcasted_iota(jnp.int32, (NX, NY), 1)
    first_row, last_row = row == 0, row == NX - 1
    first_col, last_col = col == 0, col == NY - 1

    def coef(c, e):
        return coef_ref[c, e - (HALO - COEF_HALO)]

    def inside(e, x):
        if e < HALO:
            return jnp.where(has_low, x, 0.0)
        if e >= HALO + LAYERS:
            return jnp.where(has_high, x, 0.0)
        return x

    def flat(x):
        down = jnp.where(first_row, 0.0, pltpu.roll(x, 1, 0))
        up = jnp.where(last_row, 0.0, pltpu.roll(x, NX - 1, 0))
        right = jnp.where(first_col, 0.0, pltpu.roll(x, 1, 1))
        left = jnp.where(last_col, 0.0, pltpu.roll(x, NY - 1, 1))
        return (down + up) + (right + left)

    for step in range(STEPS):
        src = (None, a_ref, b_ref, a_ref)[step]
        dst = (a_ref, b_ref, a_ref, None)[step]

        def load(f, e):
            if src is None:
                return inside(e, state_ref[f, e])
            return src[f, e]

        for e in range(step + 1, EXT - 1 - step):
            m, v, h, c = (load(f, e) for f in range(FIELDS))
            mu, vu, hu, cu = (load(f, e - 1) for f in range(FIELDS))
            ml, vl, hl, cl = (load(f, e + 1) for f in range(FIELDS))
            diffuse, reacts, permeab = coef(0, e), coef(1, e), coef(2, e)
            vp = advect_coef * jnp.maximum(v, 0.0)
            vn = advect_coef * jnp.minimum(v, 0.0)

            def transport(q, qu, ql):
                return vp * (q - qu) + vn * (ql - q)

            def laplace(q, qu, ql):
                return qu + ql + flat(q) - 6.0 * q

            melting = reacts * (h - 0.5 * c)
            new = (
                m - transport(m, mu, ml) + melting,
                v + 0.2 * (permeab * jnp.tanh(m) - v) + 0.1 * laplace(v, vu, vl),
                h - transport(h, hu, hl) + diffuse * laplace(h, hu, hl) - 0.5 * melting,
                c - transport(c, cu, cl) + diffuse * laplace(c, cu, cl),
            )
            for f in range(FIELDS):
                if dst is None:
                    out_ref[f, e - HALO] = new[f]
                else:
                    dst[f, e] = inside(e, new[f])


def local(ancestors, ensemble, diffusivity, melting_speed, permeability):
    any_spec = pl.BlockSpec(memory_space=pl.ANY)
    tiles = ensemble.reshape(HOLDERS, TILE, NY)
    split = (LAYERS, NX // TILE, TILE, NY)
    coefs = [c.reshape(split) for c in (diffusivity, melting_speed, permeability)]
    dma = pltpu.SemaphoreType.DMA
    state, coefs = pl.pallas_call(
        resample_kernel,
        out_shape=(
            pltpu.VMEM((FIELDS, EXT, NX // TILE, TILE, NY), jnp.float32),
            pltpu.VMEM((3, LAYERS + 2 * COEF_HALO, NX // TILE, TILE, NY), jnp.float32),
        ),
        in_specs=[pl.BlockSpec(memory_space=pltpu.SMEM)] + [any_spec] * 4,
        out_specs=(pl.BlockSpec(memory_space=pltpu.VMEM),) * 2,
        scratch_shapes=[
            pltpu.VMEM((DOM, TILE, NY), jnp.float32),
            pltpu.VMEM((DOM, TILE, NY), jnp.float32),
            pltpu.VMEM((HOLDERS, TILE, NY), jnp.float32),
            dma,
            pltpu.VMEM((2, 1, 128), jnp.int32),
            pltpu.VMEM((2, 8, 1, 128), jnp.int32),
            pltpu.VMEM((1, 128), jnp.int32),
            pltpu.SMEM((1, 128), jnp.int32),
            dma((4,)),
            dma,
            dma,
            dma,
            dma((1,)),
            dma,
            dma((FIELDS,)),
            dma((2, FIELDS)),
            dma((2, FIELDS)),
            dma((2, 3)),
            dma((2, 3)),
            dma((3,)),
            pltpu.SemaphoreType.REGULAR,
        ],
        compiler_params=pltpu.CompilerParams(collective_id=0, has_side_effects=True),
    )(ancestors, tiles, *coefs)
    state = state.reshape(FIELDS, EXT, NX, NY)
    coefs = coefs.reshape(3, LAYERS + 2 * COEF_HALO, NX, NY)
    vmem = pl.BlockSpec(memory_space=pltpu.VMEM)
    pin, space = pltpu.with_memory_space_constraint, pltpu.VMEM
    out = pl.pallas_call(
        forecast_kernel,
        out_shape=jax.ShapeDtypeStruct((FIELDS, LAYERS, NX, NY), jnp.float32),
        in_specs=[vmem] * 2,
        out_specs=vmem,
        scratch_shapes=[pltpu.VMEM((FIELDS, EXT, NX, NY), jnp.float32)] * 2,
    )(pin(state, space), pin(coefs, space))
    return out[None]


def solution(mesh):
    return jax.shard_map(
        local,
        mesh=mesh,
        in_specs=(
            P("dom"),
            P("dom", None, "depth", None, None),
            P("depth", None, None),
            P("depth", None, None),
            P("depth", None, None),
        ),
        out_specs=P("dom", None, "depth", None, None),
        check_vma=False,
    )
```

```python
import jax
import jax.numpy as jnp
from jax import lax
from jax.experimental import pallas as pl
from jax.experimental.pallas import tpu as pltpu
from jax.sharding import PartitionSpec as P

STEPS = 4
FIELDS = 4
DOM = 64
DEPTH = 8
LAYERS = 6
NX = 16
NY = 128
TILE = 8
HOLDERS = FIELDS * LAYERS * NX // TILE
HALO = STEPS
EXT = LAYERS + 2 * HALO
COEF_HALO = STEPS - 1

advect_coef = 0.1


def remote(src, dst, send_sem, recv_sem, **where):
    return pltpu.make_async_remote_copy(
        src_ref=src,
        dst_ref=dst,
        send_sem=send_sem,
        recv_sem=recv_sem,
        device_id=where,
        device_id_type=pl.DeviceIdType.MESH,
    )


def split_dom(index):
    return index // 8, lax.rem(index // 4, 2), lax.rem(index, 4)


def join_dom(y, z_hi, x):
    return y * 8 + z_hi * 4 + x


def resample_kernel(
    anc_ref,
    ens_ref,
    dif_ref,
    spd_ref,
    per_ref,
    state_ref,
    coef_ref,
    held,
    chosen,
    mine,
    mine_sem,
    anc_send,
    anc_recv,
    anc_row,
    anc_all,
    anc_sems,
    smem_sem,
    p1_send,
    p1_recv,
    local_sem,
    p2_send,
    p2_recv,
    halo_send,
    halo_recv,
    coef_send,
    coef_recv,
    own_coef_sem,
    cross,
):
    me = lax.axis_index("dom")
    dp = lax.axis_index("depth")
    my_y, my_z, my_x = split_dom(me)
    near = (my_y + 2) & 7
    late_holder = ((my_x != 2) & (near < 5)) | ((my_x == 2) & (my_y == 0))
    late_tile = jnp.where(my_x == 2, HOLDERS - 1, DOM // 2 + near * 3 + my_x - my_x // 3)
    my_tile = jnp.where(my_z == 0, my_y * 4 + my_x, late_tile)
    is_holder = (my_z == 0) | late_holder
    has_low = dp > 0
    has_high = dp < DEPTH - 1

    fetch = pltpu.make_async_copy(ens_ref, mine, mine_sem)
    fetch.start()
    coefs = (dif_ref, spd_ref, per_ref)
    own_coefs = [
        pltpu.make_async_copy(
            coefs[c], coef_ref.at[c, pl.ds(COEF_HALO, LAYERS)], own_coef_sem.at[c]
        )
        for c in range(3)
    ]
    barrier = pltpu.get_barrier_semaphore()

    def greet(t, carry):
        pl.semaphore_signal(
            barrier,
            inc=1,
            device_id={"dom": me ^ t},
            device_id_type=pl.DeviceIdType.MESH,
        )
        return carry

    for t in (4, 5, 3, 6, 2, 7, 1):
        greet(8 * t, 0)
    for t in (2, 3, 1):
        greet(t, 0)

    @pl.when(my_z == 0)
    def _():
        def greet_late(t, carry):
            for k in range(4):
                greet(t * 8 + 4 + k, 0)
            return carry

        lax.fori_loop(0, 8, greet_late, 0)

    @pl.when(has_low)
    def _():
        pl.semaphore_signal(
            barrier, inc=1, device_id={"depth": dp - 1}, device_id_type=pl.DeviceIdType.MESH
        )

    @pl.when(has_high)
    def _():
        pl.semaphore_signal(
            barrier, inc=1, device_id={"depth": dp + 1}, device_id_type=pl.DeviceIdType.MESH
        )

    lane = lax.broadcasted_iota(jnp.int32, (1, 128), 1)
    anc_send[0] = jnp.where(lane == me, anc_ref[0], 0)
    pl.semaphore_wait(
        barrier,
        10
        + DOM // 2 * my_z
        + has_low.astype(jnp.int32)
        + has_high.astype(jnp.int32),
    )

    def anc_hop(hop, stride):
        for t in range(1, 8):
            remote(
                anc_send.at[hop],
                anc_recv.at[hop, t],
                anc_sems.at[2 * hop],
                anc_sems.at[2 * hop + 1],
                dom=me ^ (t * stride),
            ).start()

    def anc_done(hop):
        view = anc_recv.at[hop, pl.ds(1, 7)]
        pltpu.make_async_copy(view, view, anc_sems.at[2 * hop + 1]).wait()
        total = anc_send[hop]
        for t in range(1, 8):
            total = total + anc_recv[hop, t]
        return total

    anc_hop(0, 8)


    def coef_to_low(c):
        return remote(
            coefs[c].at[pl.ds(0, COEF_HALO)],
            coef_ref.at[c, pl.ds(COEF_HALO + LAYERS, COEF_HALO)],
            coef_send.at[0, c],
            coef_recv.at[1, c],
            depth=dp - 1,
        )

    def coef_to_high(c):
        return remote(
            coefs[c].at[pl.ds(LAYERS - COEF_HALO, COEF_HALO)],
            coef_ref.at[c, pl.ds(0, COEF_HALO)],
            coef_send.at[1, c],
            coef_recv.at[0, c],
            depth=dp + 1,
        )

    def start_coefs():
        for copy in own_coefs:
            copy.start()

        @pl.when(has_low)
        def _():
            for c in range(3):
                coef_to_low(c).start()

        @pl.when(has_high)
        def _():
            for c in range(3):
                coef_to_high(c).start()

    @pl.when(my_z == 0)
    def _():
        start_coefs()

    turn = 1 - 2 * (dp & 1)

    def send_tile(p, target):
        @pl.when(target != me)
        def _():
            remote(mine.at[p], held.at[me], p1_send, p1_recv, dom=target).start()

    def spread_early():
        def body(t, carry):
            y = (my_y + 12 + t * turn) & 7
            for k in range(4):
                x = my_x ^ k
                send_tile(y * 4 + x, join_dom(y, 0, x))
            return carry

        lax.fori_loop(0, 8, body, 0)

    def spread_late():
        def body(t, carry):
            for i in range(3):
                send_tile(DOM // 2 + t * 3 + i, join_dom((t + 6) & 7, 1, i + i // 2))
            return carry

        lax.fori_loop(0, 5, body, 0)
        send_tile(HOLDERS - 1, join_dom(0, 1, 2))

    fetch.wait()

    @pl.when(my_z == 1)
    def _():
        for k in range(4):
            pl.semaphore_signal(
                cross,
                inc=1,
                device_id={"dom": me ^ (4 + k)},
                device_id_type=pl.DeviceIdType.MESH,
            )
        spread_early()

    anc_send[1] = anc_done(0)

    @pl.when(my_z == 0)
    def _():
        spread_early()
        pl.semaphore_wait(cross, 4)

    anc_hop(1, 1)
    spread_late()

    own_plane = pltpu.make_async_copy(mine.at[my_tile], held.at[me], local_sem.at[0])

    @pl.when(is_holder)
    def _():
        own_plane.start()


    @pl.when(my_z == 1)
    def _():
        start_coefs()

    anc_row[...] = anc_done(1)
    to_smem = pltpu.make_async_copy(anc_row, anc_all, smem_sem)
    to_smem.start()
    to_smem.wait()

    f = my_tile // (2 * LAYERS)
    layer = HALO + lax.rem(my_tile, 2 * LAYERS) // 2
    half = lax.rem(my_tile, 2)

    @pl.when(is_holder)
    def _():
        others = held.at[pl.ds(0, DOM - 1)]
        pltpu.make_async_copy(others, others, p1_recv).wait()
        own_plane.wait()
        place = state_ref.at[f, layer, half]

        def send(n, target):
            chosen[n] = held[anc_all[0, target]]
            remote(chosen.at[n], place, p2_send, p2_recv.at[f], dom=target).start()

        def give(z, mine_first):
            def body(t, carry):
                y = (my_y + 8 + t * turn) & 7
                for k in range(4):
                    send(z * 32 + t * 4 + k, join_dom(y, z, my_x ^ k))
                return carry

            if mine_first:
                n = z * 32
                chosen[n] = held[anc_all[0, me]]
                pltpu.make_async_copy(chosen.at[n], place, p2_recv.at[f]).start()
                for k in range(1, 4):
                    send(n + k, join_dom(my_y, z, my_x ^ k))
            lax.fori_loop(1 if mine_first else 0, 8, body, 0)

        @pl.when(my_z == 0)
        def _():
            give(0, True)
            give(1, False)

        @pl.when(my_z == 1)
        def _():
            give(0, False)
            give(1, True)

    def to_low(field):
        return remote(
            state_ref.at[field, pl.ds(HALO, HALO)],
            state_ref.at[field, pl.ds(HALO + LAYERS, HALO)],
            halo_send.at[0, field],
            halo_recv.at[1, field],
            depth=dp - 1,
        )

    def to_high(field):
        return remote(
            state_ref.at[field, pl.ds(LAYERS, HALO)],
            state_ref.at[field, pl.ds(0, HALO)],
            halo_send.at[1, field],
            halo_recv.at[0, field],
            depth=dp + 1,
        )

    for field in range(FIELDS):
        own = held.at[pl.ds(0, HOLDERS // FIELDS)]
        pltpu.make_async_copy(own, own, p2_recv.at[field]).wait()

        @pl.when(has_low)
        def _(field=field):
            to_low(field).start()

        @pl.when(has_high)
        def _(field=field):
            to_high(field).start()

    @pl.when(is_holder)
    def _():
        sent = held.at[pl.ds(0, HOLDERS - 1)]
        pltpu.make_async_copy(sent, sent, p1_send).wait()
        sent = chosen.at[pl.ds(0, DOM - 1)]
        pltpu.make_async_copy(sent, sent, p2_send).wait()

    @pl.when(jnp.logical_not(is_holder))
    def _():
        sent = held.at[pl.ds(0, HOLDERS)]
        pltpu.make_async_copy(sent, sent, p1_send).wait()

    for copy in own_coefs:
        copy.wait()

    for hop in range(2):
        view = anc_recv.at[hop, pl.ds(1, 7)]
        pltpu.make_async_copy(view, view, anc_sems.at[2 * hop]).wait()

    @pl.when(has_low)
    def _():
        for c in range(3):
            coef_to_low(c).wait_send()
            coef_to_high(c).wait_recv()
        for field in range(FIELDS):
            to_low(field).wait_send()
            to_high(field).wait_recv()

    @pl.when(has_high)
    def _():
        for c in range(3):
            coef_to_high(c).wait_send()
            coef_to_low(c).wait_recv()
        for field in range(FIELDS):
            to_high(field).wait_send()
            to_low(field).wait_recv()


def forecast_kernel(state_ref, coef_ref, out_ref, a_ref, b_ref):
    dp = lax.axis_index("depth")
    has_low = dp > 0
    has_high = dp < DEPTH - 1
    row = lax.broadcasted_iota(jnp.int32, (NX, NY), 0)
    col = lax.broadcasted_iota(jnp.int32, (NX, NY), 1)
    first_row, last_row = row == 0, row == NX - 1
    first_col, last_col = col == 0, col == NY - 1

    def coef(c, e):
        return coef_ref[c, e - (HALO - COEF_HALO)]

    def inside(e, x):
        if e < HALO:
            return jnp.where(has_low, x, 0.0)
        if e >= HALO + LAYERS:
            return jnp.where(has_high, x, 0.0)
        return x

    def flat(x):
        down = jnp.where(first_row, 0.0, pltpu.roll(x, 1, 0))
        up = jnp.where(last_row, 0.0, pltpu.roll(x, NX - 1, 0))
        right = jnp.where(first_col, 0.0, pltpu.roll(x, 1, 1))
        left = jnp.where(last_col, 0.0, pltpu.roll(x, NY - 1, 1))
        return (down + up) + (right + left)

    for step in range(STEPS):
        src = (None, a_ref, b_ref, a_ref)[step]
        dst = (a_ref, b_ref, a_ref, None)[step]

        def load(f, e):
            if src is None:
                return inside(e, state_ref[f, e])
            return src[f, e]

        for e in range(step + 1, EXT - 1 - step):
            m, v, h, c = (load(f, e) for f in range(FIELDS))
            mu, vu, hu, cu = (load(f, e - 1) for f in range(FIELDS))
            ml, vl, hl, cl = (load(f, e + 1) for f in range(FIELDS))
            diffuse, reacts, permeab = coef(0, e), coef(1, e), coef(2, e)
            vp = advect_coef * jnp.maximum(v, 0.0)
            vn = advect_coef * jnp.minimum(v, 0.0)

            def transport(q, qu, ql):
                return vp * (q - qu) + vn * (ql - q)

            def laplace(q, qu, ql):
                return qu + ql + flat(q) - 6.0 * q

            melting = reacts * (h - 0.5 * c)
            new = (
                m - transport(m, mu, ml) + melting,
                v + 0.2 * (permeab * jnp.tanh(m) - v) + 0.1 * laplace(v, vu, vl),
                h - transport(h, hu, hl) + diffuse * laplace(h, hu, hl) - 0.5 * melting,
                c - transport(c, cu, cl) + diffuse * laplace(c, cu, cl),
            )
            for f in range(FIELDS):
                if dst is None:
                    out_ref[f, e - HALO] = new[f]
                else:
                    dst[f, e] = inside(e, new[f])


def local(ancestors, ensemble, diffusivity, melting_speed, permeability):
    any_spec = pl.BlockSpec(memory_space=pl.ANY)
    tiles = ensemble.reshape(HOLDERS, TILE, NY)
    split = (LAYERS, NX // TILE, TILE, NY)
    coefs = [c.reshape(split) for c in (diffusivity, melting_speed, permeability)]
    dma = pltpu.SemaphoreType.DMA
    state, coefs = pl.pallas_call(
        resample_kernel,
        out_shape=(
            pltpu.VMEM((FIELDS, EXT, NX // TILE, TILE, NY), jnp.float32),
            pltpu.VMEM((3, LAYERS + 2 * COEF_HALO, NX // TILE, TILE, NY), jnp.float32),
        ),
        in_specs=[pl.BlockSpec(memory_space=pltpu.SMEM)] + [any_spec] * 4,
        out_specs=(pl.BlockSpec(memory_space=pltpu.VMEM),) * 2,
        scratch_shapes=[
            pltpu.VMEM((DOM, TILE, NY), jnp.float32),
            pltpu.VMEM((DOM, TILE, NY), jnp.float32),
            pltpu.VMEM((HOLDERS, TILE, NY), jnp.float32),
            dma,
            pltpu.VMEM((2, 1, 128), jnp.int32),
            pltpu.VMEM((2, 8, 1, 128), jnp.int32),
            pltpu.VMEM((1, 128), jnp.int32),
            pltpu.SMEM((1, 128), jnp.int32),
            dma((4,)),
            dma,
            dma,
            dma,
            dma((1,)),
            dma,
            dma((FIELDS,)),
            dma((2, FIELDS)),
            dma((2, FIELDS)),
            dma((2, 3)),
            dma((2, 3)),
            dma((3,)),
            pltpu.SemaphoreType.REGULAR,
        ],
        compiler_params=pltpu.CompilerParams(collective_id=0, has_side_effects=True),
    )(ancestors, tiles, *coefs)
    state = state.reshape(FIELDS, EXT, NX, NY)
    coefs = coefs.reshape(3, LAYERS + 2 * COEF_HALO, NX, NY)
    vmem = pl.BlockSpec(memory_space=pltpu.VMEM)
    pin, space = pltpu.with_memory_space_constraint, pltpu.VMEM
    out = pl.pallas_call(
        forecast_kernel,
        out_shape=jax.ShapeDtypeStruct((FIELDS, LAYERS, NX, NY), jnp.float32),
        in_specs=[vmem] * 2,
        out_specs=vmem,
        scratch_shapes=[pltpu.VMEM((FIELDS, EXT, NX, NY), jnp.float32)] * 2,
    )(pin(state, space), pin(coefs, space))
    return out[None]


def solution(mesh):
    return jax.shard_map(
        local,
        mesh=mesh,
        in_specs=(
            P("dom"),
            P("dom", None, "depth", None, None),
            P("depth", None, None),
            P("depth", None, None),
            P("depth", None, None),
        ),
        out_specs=P("dom", None, "depth", None, None),
        check_vma=False,
    )
```
